32 devices in a mesh: rx: 8 (over z, x), ry: 4 (over y, core).
Axes of the slice: x: 2, y: 2, z: 4, core: 2. Of those that a mesh axis runs over, the one named last changes fastest.
Arguments:
- clean: bfloat16 [8, 4, 4, 2, 192, 1024], P('rx', 'ry'), may hold values from -6 to 6
- noise: bfloat16 [8, 4, 4, 2, 192, 1024], P('rx', 'ry'), may hold values from -6 to 6
- noise_level: int32 [8, 4, 4, 2], P('rx', 'ry'), may hold values from 0 to 31
- weight: float32 [8, 4, 9, 192, 192], P('rx', 'ry'), may hold values from -6 to 6
- velocity: float32 [8, 4, 9, 192, 192], P('rx', 'ry'), may hold values from -0.6 to 0.6
Outputs:
- new_weight: float32 [8, 4, 9, 192, 192], P('rx', 'ry')
- new_velocity: float32 [8, 4, 9, 192, 192], P('rx', 'ry')
The draws below stay inside these ranges and needn't reach their ends.
All inputs are finite; a program needn't handle non-finite values.
Results may differ from the reference program's by a relative error of at most 0.0066.
Values sent between devices are 32-bit elements; how exact they have to be, the bound alone decides.
No kernel may reach another device: no remote copies, remote signals or barrier semaphores. Data moves between devices by JAX's collectives and lax.ppermute only.
A program may use at most 192 MiB of HBM per device.

```python
import math
import jax
import jax.numpy as jnp
from jax import lax

C = 192
RES = 32
BATCH = 2
STEPS = 4
LEVELS = 32
N_RX = 8
N_RY = 4


def place_ends(entries, rng, smallest, largest):
    extent = entries.shape
    index_at = [jax.random.randint(jax.random.fold_in(rng, axis), (), 0, extent[axis]) for axis in range(len(extent))]
    entries = entries.at[tuple(index_at)].set(smallest)
    longest = extent.index(max(extent))
    index_at[longest] = (index_at[longest] + 1) % extent[longest]
    return entries.at[tuple(index_at)].set(largest)


def shard_levels(key, dims, pieces, least, largest):
    def one(axis_at, shards_of):
        draws = jax.random.uniform(jax.random.fold_in(jax.random.fold_in(key, 6), axis_at), (shards_of,), jnp.float32, least / len(pieces), largest / len(pieces))
        return jnp.repeat(jnp.exp(draws), dims[axis_at] // shards_of).reshape((-1,) + (1,) * (len(dims) - axis_at - 1))

    factor_of = one(*pieces[0])
    for cut in pieces[1:]:
        factor_of = factor_of * one(*cut)
    return factor_of


def scatter_about(key, dims, spread, reach, split=(), kind=jnp.bfloat16):
    loudness = shard_levels(key, dims, split, -0.22, 0.18) if split else 1.0
    drawn = jax.random.normal(key, dims, jnp.float32) * spread * loudness
    return jnp.minimum(jnp.maximum(drawn, -reach), reach).astype(kind)


def setup_inputs(seed: int = 0) -> dict:
    key_list = jax.random.split(jax.random.key(seed), 6)
    return {
        "clean": scatter_about(key_list[0], (N_RX, N_RY, STEPS, BATCH, C, RES * RES), 1.0, 6.0, ((0, 8), (1, 4))),
        "noise": scatter_about(key_list[1], (N_RX, N_RY, STEPS, BATCH, C, RES * RES), 1.0, 6.0, ((0, 8), (1, 4))),
        "noise_level": place_ends(jax.random.randint(key_list[2], (N_RX, N_RY, STEPS, BATCH), 0, LEVELS), jax.random.fold_in(key_list[2], 1), 0, LEVELS - 1).astype(jnp.int32),
        "weight": scatter_about(key_list[3], (N_RX, N_RY, 9, C, C), 1.0, 6.0, ((0, 8), (1, 4)), jnp.float32),
        "velocity": scatter_about(key_list[4], (N_RX, N_RY, 9, C, C), 0.1, 0.6, ((0, 8), (1, 4)), jnp.float32),
    }


norm_epsilon = 1e-05
momentum_decay = 0.9
learn_rate = 50.0
silu_scale = 0.596

def prepare(weight):
    fan = weight.shape[0] * weight.shape[1]
    mean_square = lax.optimization_barrier(jnp.mean(weight * weight, axis=(0, 1)))
    radius = jnp.sqrt(mean_square + norm_epsilon)
    w_eff = (weight / (radius * math.sqrt(fan))).astype(jnp.bfloat16)
    return (w_eff.reshape(fan, weight.shape[2]), radius)

def columns(latents):
    batch_rows, channels, cells = latents.shape
    grid = latents.reshape(batch_rows, channels, RES, RES)
    padded = jnp.pad(grid, ((0, 0), (0, 0), (1, 1), (1, 1)))
    taps = [padded[:, :, row:row + RES, col:col + RES] for row in range(3) for col in range(3)]
    return jnp.stack(taps, axis=1).reshape(batch_rows, 9 * channels, cells)

def input_columns(clean_s, noise_s, level_s):
    sigma = 0.2 * 25.0 ** (level_s.astype(jnp.float32) / (LEVELS - 1))
    c_in = 1.0 / jnp.sqrt(sigma * sigma + 0.25)
    noisy = c_in[:, None, None] * (clean_s.astype(jnp.float32) + sigma[:, None, None] * noise_s.astype(jnp.float32))
    return columns(noisy.astype(jnp.bfloat16))

def out_grad(w_flat, cols, clean_s, norm_count):
    z_value = jnp.einsum('kc,bkp->bcp', w_flat, cols, preferred_element_type=jnp.float32)
    sig = jax.nn.sigmoid(z_value)
    pred = z_value * sig / silu_scale
    error = pred - clean_s.astype(jnp.float32)
    return (2.0 * error * sig * (1.0 + z_value * (1.0 - sig)) / (silu_scale * norm_count)).astype(jnp.bfloat16)

def raw_grad(grad_eff, weight, radius):
    fan = weight.shape[0] * weight.shape[1]
    inner = lax.optimization_barrier(jnp.sum(grad_eff * weight, axis=(0, 1)))
    return (grad_eff / radius - weight * inner / (fan * radius ** 3)) / math.sqrt(fan)

def local_step(weight, velocity, clean_s, noise_s, level_s):
    w_flat, radius = prepare(weight)
    norm_count = clean_s.shape[0] * clean_s.shape[2]
    cols = input_columns(clean_s, noise_s, level_s)
    dz_value = out_grad(w_flat, cols, clean_s, norm_count)
    grad_eff = jnp.einsum('bkp,bcp->kc', cols, dz_value, preferred_element_type=jnp.float32).reshape(weight.shape)
    grad = raw_grad(grad_eff, weight, radius)
    velocity = momentum_decay * velocity + learn_rate * grad
    return (weight - velocity, velocity)

def partner_first(array, distance):
    total = array.shape[0]
    blocks = array.reshape((total // (2 * distance), 2, distance) + array.shape[1:])
    return jnp.flip(blocks, axis=1).reshape(array.shape)

def reference(clean, noise, noise_level, weight, velocity):
    n_first, n_second = (weight.shape[0], weight.shape[1])
    replicas = n_first * n_second
    for step in range(STEPS):

        def per_replica(items):
            return local_step(*items)
        flat = (weight.reshape((replicas,) + weight.shape[2:]), velocity.reshape((replicas,) + velocity.shape[2:]), clean[:, :, step].reshape((replicas,) + clean.shape[3:]), noise[:, :, step].reshape((replicas,) + noise.shape[3:]), noise_level[:, :, step].reshape((replicas,) + noise_level.shape[3:]))
        local, velocity_flat = lax.map(per_replica, flat)
        local = local.reshape(weight.shape)
        velocity = velocity_flat.reshape(velocity.shape)
        if step % 2 == 0:
            distance = n_first // 2 ** (1 + step // 2)
            other = partner_first(local, distance)
        else:
            distance = n_second // 2 ** (1 + step // 2)
            other = jnp.swapaxes(partner_first(jnp.swapaxes(local, 0, 1), distance), 0, 1)
        weight = 0.5 * (local + other)
    return (weight, velocity)
```

```python
import functools
import math

import jax
import jax.numpy as jnp
from jax import lax
from jax.experimental import pallas as pl
from jax.experimental.pallas import tpu as pltpu
from jax.sharding import PartitionSpec as P


LEVELS = 32
CHANNELS = 192
LANES = 128
DY = 3

norm_epsilon = 1e-05
momentum_decay = 0.9
learn_rate = 50.0
silu_scale = 0.596


def chunk_plan(channels):
    if channels == 192:
        return (64, 64, 48, 16)
    plan = []
    left = channels
    while left:
        take = min(64, left)
        plan.append(take)
        left -= take
    return tuple(plan)


def partner(shard, axis, bit):
    return lax.ppermute(shard, axis, [(i, i ^ 1 << bit) for i in range(lax.axis_size(axis))])


def exchange(array, step):
    axis = "rx" if step % 2 == 0 else "ry"
    return partner(array, axis, lax.axis_size(axis).bit_length() - 2 - step // 2)


def whole_lanes(width):
    return width // LANES * LANES


def packed_rows(rows, width):
    return rows * width // LANES


def pack_into(ref, value):
    rows, width = value.shape
    full = whole_lanes(width)
    for k in range(full // LANES):
        ref[k * rows : (k + 1) * rows, :] = value[:, k * LANES : (k + 1) * LANES]
    if width > full:
        half = rows // 2
        tail = value[:, full:]
        base = full // LANES * rows
        ref[base : base + half, :] = jnp.concatenate([tail[:half], tail[half:]], axis=1)


def unpack_mean(one, two, out, rows, width):
    full = whole_lanes(width)
    for k in range(full // LANES):
        at = slice(k * rows, (k + 1) * rows)
        out[:, k * LANES : (k + 1) * LANES] = 0.5 * (one[at, :] + two[at, :])
    if width > full:
        half = rows // 2
        at = slice(full // LANES * rows, full // LANES * rows + half)
        tail = 0.5 * (one[at, :] + two[at, :])
        out[:half, full:] = tail[:, : LANES // 2]
        out[half:, full:] = tail[:, LANES // 2 :]


def lane_shift(value, amount):
    return pltpu.roll(value, (-amount) % value.shape[1], axis=1)


def cell_index(cells):
    return lax.broadcasted_iota(jnp.int32, (1, cells), 1)


def side_of(cells):
    return math.isqrt(cells)


def make_noisy(level, clean, noise):
    cells = clean.shape[1]
    side = side_of(cells)
    exponent = level.astype(jnp.float32) / (LEVELS - 1)
    sigma = 0.2 * jnp.exp(exponent * math.log(25.0))
    c_in = 1.0 / jnp.sqrt(sigma * sigma + 0.25)
    sigma = jnp.broadcast_to(sigma, (1, cells))
    c_in = jnp.broadcast_to(c_in, (1, cells))
    noisy = c_in * (clean.astype(jnp.float32) + sigma * noise.astype(jnp.float32))
    across = cell_index(cells) % side
    shifts = (read(noisy, -1, across >= 1), noisy, read(noisy, 1, across < side - 1))
    return jnp.concatenate([part.astype(jnp.bfloat16) for part in shifts], axis=0)


def latent_kernel(level_ref, clean_in, noise_in, _, x_ref, xt_ref, clean_ref, turn_ref, *, step):
    turn_ref[...] = jnp.zeros_like(turn_ref)
    for batch in range(clean_in.shape[0]):
        level = level_ref[0, 0, step : step + 1, batch : batch + 1]
        noisy = make_noisy(level, clean_in[batch], noise_in[batch])
        x_ref[batch] = noisy
        xt_ref[batch] = jnp.transpose(noisy)
        clean_ref[batch] = clean_in[batch]


def turn_kernel(*refs, plan):
    w_in, v_in = refs[:2]
    outs = refs[3:-1]
    refs[-1][...] = jnp.zeros_like(refs[-1])
    _, channels, lanes = w_in.shape
    for dy in range(DY):
        for k, source in enumerate((w_in, v_in)):
            piece = source[DY * dy : DY * dy + DY].reshape(DY * channels, lanes)
            turned = jnp.transpose(piece)
            for out, (offset, count) in zip(outs[k::2], plan):
                out[dy * count : (dy + 1) * count, :] = turned[offset : offset + count]


def tap_sums(value, count):
    total = jnp.sum(value, axis=1, keepdims=True)
    return sum(total[k * count : (k + 1) * count] for k in range(DY))


def read(value, amount, valid):
    return jnp.where(valid, lane_shift(value, amount), 0.0)


def rows_down(value, side):
    moved = lane_shift(value, -side)
    head = jnp.where(cell_index(LANES) >= side, moved[:, :LANES], 0.0)
    return jnp.concatenate([head, moved[:, LANES:]], axis=1)


def rows_up(value, side):
    moved = lane_shift(value, side)
    tail = jnp.where(cell_index(LANES) < LANES - side, moved[:, -LANES:], 0.0)
    return jnp.concatenate([moved[:, :-LANES], tail], axis=1)


def step_kernel(*refs, first, start):
    refs = list(refs)
    if first:
        w_full = refs.pop(0)
    else:
        own, recv = refs.pop(0), refs.pop(0)
    v_in, clean_ref, x_ref, xt_ref, _, local_ref, v_out, token = refs[:8]
    scratch = refs[8:]
    token[...] = jnp.zeros_like(token)
    if not first:
        w_full = scratch[0]
    w_half, grad_ref = scratch[-2:]
    rows, width = w_full.shape
    count = rows // DY
    batches, _, cells = x_ref.shape
    side = side_of(cells)
    fan = DY * width

    if not first:
        unpack_mean(own, recv, w_full, rows, width)
    weight = w_full[...]
    radius = jnp.sqrt(tap_sums(weight * weight, count) / fan + norm_epsilon)
    inverse = 1.0 / (radius * math.sqrt(fan))
    for tap in range(DY):
        at = slice(tap * count, (tap + 1) * count)
        w_half[at, :] = (weight[at] * inverse).astype(jnp.bfloat16)

    w_value = w_half[...]

    def one_latent(batch):
        part = jnp.dot(w_value, x_ref[batch], preferred_element_type=jnp.float32)
        z_value = (
            part[count : 2 * count]
            + rows_down(part[:count], side)
            + rows_up(part[2 * count :], side)
        )
        sig = 1.0 / (1.0 + jnp.exp(-z_value))
        clean = clean_ref[batch, start : start + count, :].astype(jnp.float32)
        error = z_value * sig * (1.0 / silu_scale) - clean
        dz_value = (
            (2.0 / (silu_scale * batches * cells)) * error * sig * (1.0 + z_value * (1.0 - sig))
        )
        spread = (rows_up(dz_value, side), dz_value, rows_down(dz_value, side))
        spread = jnp.concatenate([piece.astype(jnp.bfloat16) for piece in spread], axis=0)
        return jnp.dot(spread, xt_ref[batch], preferred_element_type=jnp.float32)

    if UNROLL:
        grad = sum(one_latent(batch) for batch in range(batches))
    else:
        grad_ref[...] = jnp.zeros_like(grad_ref)

        def add_latent(batch, carry):
            grad_ref[...] += one_latent(batch)
            return carry

        lax.fori_loop(0, batches, add_latent, 0)
        grad = grad_ref[...]
    weight = w_full[...]
    inner = tap_sums(grad * weight, count)
    g_scale = learn_rate * inverse
    w_scale = learn_rate * inner * inverse / (fan * radius * radius)
    g_scale = jnp.concatenate([g_scale] * DY, axis=0)
    w_scale = jnp.concatenate([w_scale] * DY, axis=0)
    velocity = momentum_decay * v_in[...] + grad * g_scale - weight * w_scale
    v_out[...] = velocity
    pack_into(local_ref, weight - velocity)


UNROLL = True
ON_CHIP = pl.BlockSpec(memory_space=pltpu.VMEM)
TOKEN = pltpu.VMEM((8, LANES), jnp.float32)
PARAMS = pltpu.CompilerParams(vmem_limit_bytes=24 * 2**20)


def run_step(step, start, count, weights, latents, token):
    first = step == 0
    x_value, xt_value, clean = latents
    width = x_value.shape[1]
    rows = DY * count
    args = [*weights, clean, x_value, xt_value, token]
    scratch = [] if first else [pltpu.VMEM((rows, width), jnp.float32)]
    scratch += [pltpu.VMEM((rows, width), jnp.bfloat16), pltpu.VMEM((rows, width), jnp.float32)]
    return pl.pallas_call(
        functools.partial(step_kernel, first=first, start=start),
        in_specs=[ON_CHIP] * len(args),
        out_specs=[ON_CHIP] * 3,
        out_shape=[
            pltpu.VMEM((packed_rows(rows, width), LANES), jnp.float32),
            pltpu.VMEM((rows, width), jnp.float32),
            TOKEN,
        ],
        scratch_shapes=scratch,
        compiler_params=PARAMS,
    )(*args)


def run_latents(step, clean, noise, level, token):
    _, _, _, batches, channels, cells = clean.shape
    latent = pl.BlockSpec(
        (None, None, None, batches, channels, cells), lambda i: (0, 0, step, 0, 0, 0)
    )
    return pl.pallas_call(
        functools.partial(latent_kernel, step=step),
        grid=(1,),
        in_specs=[ON_CHIP, latent, latent, ON_CHIP],
        out_specs=[ON_CHIP] * 4,
        out_shape=[
            pltpu.VMEM((batches, DY * channels, cells), jnp.bfloat16),
            pltpu.VMEM((batches, cells, DY * channels), jnp.bfloat16),
            pltpu.VMEM((batches, channels, cells), jnp.bfloat16),
            TOKEN,
        ],
        compiler_params=PARAMS,
    )(level, clean, noise, token)


def run_turn(block, plan, weight, velocity, token):
    taps, channels, _ = weight.shape
    spec = pl.BlockSpec((taps, channels, LANES), lambda i: (0, 0, block))
    shapes = [pltpu.VMEM((DY * count, taps // DY * channels), jnp.float32) for _, count in plan]
    return pl.pallas_call(
        functools.partial(turn_kernel, plan=plan),
        grid=(1,),
        in_specs=[spec, spec, ON_CHIP],
        out_specs=[ON_CHIP] * (2 * len(plan) + 1),
        out_shape=[shape for shape in shapes for _ in range(2)] + [TOKEN],
        compiler_params=PARAMS,
    )(weight, velocity, token)


def put_natural(out, source, at, count):
    channels = out.shape[1]
    for dy in range(DY):
        turned = jnp.transpose(source[dy * count : (dy + 1) * count, :])
        out[DY * dy : DY * dy + DY, :, at : at + count] = turned.reshape(DY, channels, count)


def finish_weight_kernel(*refs, counts, aliased):
    w_out, scratch = refs[-2:]
    at = 0
    for i, count in enumerate(counts):
        rows = DY * count
        unpack_mean(refs[2 * i], refs[2 * i + 1], scratch.at[:rows], rows, scratch.shape[1])
        put_natural(w_out, scratch, at, count)
        at += count


def finish_velocity_kernel(*refs, counts, aliased):
    v_out = refs[-1]
    at = 0
    for i, count in enumerate(counts):
        put_natural(v_out, refs[i], at, count)
        at += count


def run_finish(kernel, block, counts, pieces, shape, before):
    taps, channels, _ = shape
    args = list(pieces)
    specs = [ON_CHIP] * len(args)
    aliases = {}
    if before is not None:
        aliases = {len(args): 0}
        args.append(before)
        specs.append(pl.BlockSpec(memory_space=pl.ANY))
    scratch = []
    if kernel is finish_weight_kernel:
        scratch = [pltpu.VMEM((DY * max(counts), DY * channels), jnp.float32)]
    return pl.pallas_call(
        functools.partial(kernel, counts=counts, aliased=before is not None),
        grid=(1,),
        in_specs=specs,
        out_specs=pl.BlockSpec((taps, channels, LANES), lambda i: (0, 0, block)),
        out_shape=jax.ShapeDtypeStruct(shape, jnp.float32),
        scratch_shapes=scratch,
        input_output_aliases=aliases,
        compiler_params=PARAMS,
    )(*args)


def job_order(steps, chunks, blocks, members):
    jobs = [("latent", 0)]
    for block in blocks:
        jobs.append(("turn", block))
        jobs += [("step", 0, chunk) for chunk in members[block]]
    jobs += [("latent", step) for step in range(1, steps)]
    for wave in range(2 * (steps - 2) + chunks):
        for step in range(steps - 1, 0, -1):
            chunk = wave - 2 * (step - 1)
            if 0 <= chunk < chunks:
                jobs.append(("step", step, chunk))
    return jobs


def chunk_layout(channels):
    counts = chunk_plan(channels)
    starts = [sum(counts[:i]) for i in range(len(counts))]
    blocks = sorted({start // LANES for start in starts})
    members = {b: [i for i in range(len(counts)) if starts[i] // LANES == b] for b in blocks}
    return counts, starts, blocks, members


def body(clean, noise, noise_level, weight, velocity):
    steps = clean.shape[2]
    channels = clean.shape[4]
    w_in, v_in = weight[0, 0], velocity[0, 0]
    counts, starts, blocks, members = chunk_layout(channels)
    chunks = len(counts)
    latents = [None] * steps
    state = [None] * chunks
    arrived = [None] * chunks

    token = jnp.zeros((8, LANES), jnp.float32)

    def turn(block, token):
        plan = tuple((starts[i] - block * LANES, counts[i]) for i in members[block])
        *turned, token = run_turn(block, plan, w_in, v_in, token)
        for k, i in enumerate(members[block]):
            state[i] = (turned[2 * k], turned[2 * k + 1])
        return token

    def latent(step, token):
        *latents[step], token = run_latents(step, clean, noise, noise_level, token)
        return token

    def advance(step, chunk, token):
        if step == 0:
            weights = state[chunk]
        else:
            local, vel = state[chunk]
            weights = (local, arrived[chunk], vel)
        local, vel, token = run_step(
            step, starts[chunk], counts[chunk], weights, latents[step], token
        )
        state[chunk] = (local, vel)
        arrived[chunk] = exchange(local, step)
        return token

    for job in job_order(steps, chunks, blocks, members):
        token = {"turn": turn, "latent": latent, "step": advance}[job[0]](*job[1:], token)

    w_out = v_out = None
    for block in blocks:
        mine = members[block]
        sizes = tuple(counts[i] for i in mine)
        v_out = run_finish(
            finish_velocity_kernel, block, sizes, [state[i][1] for i in mine],
            w_in.shape, v_out,
        )
        w_out = run_finish(
            finish_weight_kernel, block, sizes,
            [a for i in mine for a in (state[i][0], arrived[i])], w_in.shape, w_out,
        )
    return (w_out[None, None], v_out[None, None])


def solution(mesh):
    in_specs = (
        P("rx", "ry", None, None, None, None),
        P("rx", "ry", None, None, None, None),
        P("rx", "ry", None, None),
        P("rx", "ry", None, None, None),
        P("rx", "ry", None, None, None),
    )
    out_specs = (P("rx", "ry", None, None, None), P("rx", "ry", None, None, None))

    _, _, _, _ = chunk_layout(CHANNELS)
    return jax.shard_map(body, mesh=mesh, in_specs=in_specs, out_specs=out_specs, check_vma=False)
```
